32 devices in a mesh: member: 8 (over z, x), domain: 4 (over y, core).
Axes of the slice: x: 2, y: 2, z: 4, core: 2. Of those that a mesh axis runs over, the one named last changes fastest.
Arguments:
- starting_tracer_fields: float32 [8, 2, 8, 64, 640], P('member', None, None, 'domain'), may hold values from -6 to 6
- surface_exchange_inputs: float32 [8, 2, 64, 640], P('member', None, 'domain'), may hold values from -4 to 4
- diffusivity: float32 [2, 8], replicated, may hold values from 0.04 to 0.2
- mixing: float32 [2, 7], replicated, may hold values from 0.02 to 0.1
- land_mask: int32 [64, 640], replicated, may hold values 0 or 1
- obs_index: int32 [4, 8, 256], P('domain'), may hold values from 0 to 1279
- obs_count: int32 [4, 8], P('domain'), may hold values from 1 to 256, as said below
- obs_value: float32 [4, 8, 256], P('domain'), may hold values from -8 to 8
- obs_error: float32 [4, 8, 256], P('domain'), may hold values from 1 to 16
Outputs:
- analysis: float32 [8, 2, 8, 64, 640], P('member', None, None, 'domain')
The draws below stay inside these ranges and needn't reach their ends.
Inputs may be any that keep to these rules, and one draw needn't show every extreme that they name: `obs_index`: A cell of the tile's 2 x 640 surface cells, counted row by row. `obs_count`: slots below the count hold observations, the rest are unused; in every domain the last tile holds exactly 256.
All inputs are finite; a program needn't handle non-finite values.
Results may differ from the reference program's by a relative error of at most 0.0001.
Values sent between devices are 32-bit elements; how exact they have to be, the bound alone decides.
A program may use at most 64 MiB of HBM per device.

```python
import math
import jax
import jax.numpy as jnp
from jax import lax

FIELDS = 2
LEVELS = 8
STEPS = 2
LON = 640
ROWS_TILE = 2
OBS_TILE = 256
MEMBERS = 8
TILES = 8
DOMAINS = 4
SUBREGION_BANDS = 16
LAT = 64


def draw_obs_count(key, part):
    tile_rank = jnp.arange(TILES, dtype=jnp.int32)
    rising = OBS_TILE // 3 + (OBS_TILE - OBS_TILE // 3) * tile_rank // max(TILES - 1, 1)
    jitter = jax.random.randint(jax.random.fold_in(key, 7), (DOMAINS, TILES), 0, OBS_TILE // 6 + 1)
    counts = jnp.clip(rising[None, :] - jitter, 1, OBS_TILE)
    return counts.at[:, TILES - 1].set(OBS_TILE).astype(jnp.int32)


def with_ends(array, own_key, low, high):
    shape = array.shape
    spot = [jax.random.randint(jax.random.fold_in(own_key, axis), (), 0, shape[axis]) for axis in range(len(shape))]
    array = array.at[tuple(spot)].set(low)
    longest = shape.index(max(shape))
    spot[longest] = (spot[longest] + 1) % shape[longest]
    return array.at[tuple(spot)].set(high)


def block_levels(own_key, extent, split, smallest, high):
    loudness = 1.0
    for axis_at, parts in split:
        draws = jax.random.uniform(jax.random.fold_in(jax.random.fold_in(own_key, 6), axis_at), (parts,), jnp.float32, smallest / len(split), high / len(split))
        loudness = loudness * jnp.repeat(jnp.exp(draws), extent[axis_at] // parts).reshape((-1,) + (1,) * (len(extent) - 1 - axis_at))
    return loudness


def normal_values(key, shape, deviation, reach, split=(), kind=jnp.bfloat16):
    entries = jax.random.normal(key, shape, jnp.float32) * deviation
    if len(split) > 0:
        entries = block_levels(key, shape, split, -0.22, 0.18) * entries
    return jnp.clip(entries, min=-reach, max=reach).astype(kind)


def setup_inputs(seed: int = 0) -> dict:
    seeds = jax.random.split(jax.random.key(seed), 10)
    return {
        "starting_tracer_fields": normal_values(seeds[0], (MEMBERS, FIELDS, LEVELS, LAT, LON), 1.0, 6.0, ((0, 8), (3, 4)), jnp.float32),
        "surface_exchange_inputs": normal_values(seeds[1], (MEMBERS, FIELDS, LAT, LON), 0.5, 4.0, ((0, 8), (2, 4)), jnp.float32),
        "diffusivity": jnp.clip(jnp.exp(jax.random.uniform(seeds[2], (FIELDS, LEVELS), jnp.float32, math.log(0.04), math.log(0.2))), 0.04, 0.2),
        "mixing": jnp.clip(jnp.exp(jax.random.uniform(seeds[3], (FIELDS, LEVELS - 1), jnp.float32, math.log(0.02), math.log(0.1))), 0.02, 0.1),
        "land_mask": with_ends((jax.random.randint(seeds[4], (LAT, LON), 0, 5) < 4).astype(jnp.int32), jax.random.fold_in(seeds[4], 1), 0, 1),
        "obs_index": with_ends(jax.random.randint(seeds[5], (DOMAINS, TILES, OBS_TILE), 0, ROWS_TILE * LON), jax.random.fold_in(seeds[5], 1), 0, (ROWS_TILE * LON) - 1).astype(jnp.int32),
        "obs_count": draw_obs_count(jax.random.fold_in(seeds[9], 71), 0),
        "obs_value": normal_values(seeds[7], (DOMAINS, TILES, OBS_TILE), 1.5, 8.0, ((0, 4),), jnp.float32),
        "obs_error": jnp.clip(jnp.exp(math.log(16.0) - 2.7725887 * jax.random.uniform(seeds[8], (DOMAINS, TILES, OBS_TILE), jnp.float32) ** block_levels(seeds[8], (DOMAINS, TILES, OBS_TILE), ((0, 4),), -0.2, 0.2)), 1.0, 16.0),
    }


def stencil(padded, mask_rows, diffusivity, mixing, surface_exchange_inputs):
    middle = padded[:, :, 1:-1]
    mask_mid = mask_rows[1:-1]
    upper_row = padded[:, :, 2:]
    lower_row = padded[:, :, :-2]
    east_cell = jnp.roll(middle, -1, axis=3)
    west_cell = jnp.roll(middle, 1, axis=3)
    lateral = mask_rows[2:] * (upper_row - middle) + mask_rows[:-2] * (lower_row - middle)
    lateral = lateral + jnp.roll(mask_mid, -1, axis=1) * (east_cell - middle)
    lateral = lateral + jnp.roll(mask_mid, 1, axis=1) * (west_cell - middle)
    downward_flux = mixing[:, :, None, None] * (middle[:, 1:] - middle[:, :-1])
    empty_level = jnp.zeros_like(middle[:, :1])
    vertical = jnp.concatenate([downward_flux, empty_level], axis=1) - jnp.concatenate([empty_level, downward_flux], axis=1)
    tendency = diffusivity[:, :, None, None] * lateral + vertical
    tendency = tendency.at[:, 0].add(surface_exchange_inputs)
    return middle + mask_mid * tendency

def partial_sums(observed, values, errors, active):
    average = lax.optimization_barrier(jnp.mean(observed, axis=0))
    anomaly = observed - average[None, :]
    weight_obs = active / errors
    gram = jnp.dot(anomaly * weight_obs[None, :], anomaly.T, precision=lax.Precision.HIGHEST)
    pull = jnp.dot(anomaly, weight_obs * (values - average), precision=lax.Precision.HIGHEST)
    return (gram, pull)

def transform(gram, pull):
    count = gram.shape[0]
    identity = jnp.eye(count, dtype=gram.dtype)
    factor = jnp.linalg.cholesky(gram + (count - 1.0) * identity)
    inverse = jax.scipy.linalg.solve_triangular(factor, identity, lower=True)
    mean_weight = jnp.dot(inverse.T, jnp.dot(inverse, pull, precision=lax.Precision.HIGHEST), precision=lax.Precision.HIGHEST)
    weights = mean_weight[:, None] + jnp.sqrt(count - 1.0) * inverse.T
    return weights - lax.optimization_barrier(jnp.mean(weights, axis=0, keepdims=True)) + 1.0 / count

def reference(starting_tracer_fields, surface_exchange_inputs, diffusivity, mixing, land_mask, obs_index, obs_count, obs_value, obs_error):
    sea_mask = land_mask.astype(jnp.float32)
    padded_mask = jnp.pad(sea_mask, ((1, 1), (0, 0)))

    def predicted_tracer_field(coordinate_couple):
        member_state, member_flux = coordinate_couple
        for _ in range(STEPS):
            padded = jnp.pad(member_state, ((0, 0), (0, 0), (1, 1), (0, 0)))
            member_state = stencil(padded, padded_mask, diffusivity, mixing, member_flux)
        return member_state
    predicted_realisations = lax.map(predicted_tracer_field, (starting_tracer_fields, surface_exchange_inputs))
    count = starting_tracer_fields.shape[0]
    pieces = []
    for subregion_offset in range(DOMAINS):
        subregion_band_slab = predicted_realisations[:, :, :, subregion_offset * SUBREGION_BANDS:(subregion_offset + 1) * SUBREGION_BANDS]
        surface = subregion_band_slab[:, 0, 0].reshape(count, -1)
        position = (jnp.arange(TILES, dtype=jnp.int32)[:, None] * (ROWS_TILE * LON) + obs_index[subregion_offset]).reshape(-1)
        observed = surface[:, position]
        active = (jnp.arange(OBS_TILE, dtype=jnp.int32)[None, :] < obs_count[subregion_offset][:, None]).astype(jnp.float32).reshape(-1)
        gram, pull = partial_sums(observed, obs_value[subregion_offset].reshape(-1), obs_error[subregion_offset].reshape(-1), active)
        kernel = transform(gram, pull)
        updated = jnp.einsum('jm,jn->mn', kernel, subregion_band_slab.reshape(count, -1), precision=lax.Precision.HIGHEST).reshape(subregion_band_slab.shape)
        local_mask = sea_mask[subregion_offset * SUBREGION_BANDS:(subregion_offset + 1) * SUBREGION_BANDS]
        pieces.append(jnp.where(local_mask > 0, updated, subregion_band_slab))
    return jnp.concatenate(pieces, axis=3)
```

```python
import functools

import jax
import jax.numpy as jnp
from jax import lax
from jax.experimental import pallas as pl
from jax.experimental.pallas import tpu as pltpu
from jax.sharding import PartitionSpec as P

STEPS = 2
SUB = 8
LANES = 128
EXACT = lax.Precision.HIGHEST
MESH = pl.DeviceIdType.MESH
NT = (((1,), (1,)), ((), ()))


def masks(mask, table):
    rows, width = mask.shape
    table[0] = mask
    table[1] = pltpu.roll(mask, rows - 1, 0)
    table[2] = pltpu.roll(mask, 1, 0)
    table[3] = pltpu.roll(mask, width - 1, 1)
    table[4] = pltpu.roll(mask, 1, 1)


def step(source, target, table, flux, diffusivity, mixing):
    fields, levels = diffusivity.shape
    rows, width = source.shape[1:]

    def one(f, carry):
        above = None
        for l in range(levels):
            x = source[f * levels + l]
            lateral = table[1] * (pltpu.roll(x, rows - 1, 0) - x)
            lateral += table[2] * (pltpu.roll(x, 1, 0) - x)
            lateral += table[3] * (pltpu.roll(x, width - 1, 1) - x)
            lateral += table[4] * (pltpu.roll(x, 1, 1) - x)
            change = diffusivity[f, l] * lateral
            if l < levels - 1:
                down = mixing[f, l] * (source[f * levels + l + 1] - x)
                change += down
            if l > 0:
                change -= above
            else:
                change += flux[f]
            above = down
            target[f * levels + l] = x + table[0] * change
        return carry

    lax.fori_loop(0, fields, one, 0)


def body(
    members, domains, x_hbm, flux_hbm, mask_hbm, index_hbm, value_hbm, error_hbm,
    count, diffusivity, mixing, out,
    x, flux, land, index, value, error, mid, fore, table,
    halo_out, halo_in, edge, edge_mid, edge_flux, edge_table,
    sent, got, rhs, sums_out, sums_in, spread, tile_mask, reply,
    load_sem, halo_send, halo_recv, fore_send, fore_recv,
    sums_send, sums_recv, reply_send, reply_recv,
):
    me = lax.axis_index("member")
    domain = lax.axis_index("domain")
    parts, rows, width = x.shape
    fields = flux.shape[0]
    chunks = got.shape[0]
    tile_rows = rows // members
    per_chunk = SUB // tile_rows
    lat = mask_hbm.shape[0]
    first = domain == 0
    last = domain == domains - 1
    start_row = pl.multiple_of(domain * rows, SUB)
    above_row = pl.multiple_of(jnp.maximum(domain * rows - SUB, 0), SUB)
    below_row = pl.multiple_of(jnp.minimum(domain * rows + rows, lat - SUB), SUB)

    loads = [
        pltpu.make_async_copy(a, b, load_sem.at[i])
        for i, (a, b) in enumerate((
            (x_hbm, x),
            (flux_hbm, flux),
            (mask_hbm.at[pl.ds(above_row, SUB)], land.at[pl.ds(0, SUB)]),
            (mask_hbm.at[pl.ds(start_row, rows)], land.at[pl.ds(SUB, rows)]),
            (mask_hbm.at[pl.ds(below_row, SUB)], land.at[pl.ds(SUB + rows, SUB)]),
            (index_hbm, index),
            (value_hbm, value),
            (error_hbm, error),
        ))
    ]
    for load in loads:
        load.start()

    barrier = pltpu.get_barrier_semaphore()

    def greet(i, carry):
        peer = lax.rem(me + i, members)
        pl.semaphore_signal(barrier, inc=1, device_id={"member": peer}, device_id_type=MESH)
        return carry

    @pl.when(jnp.logical_not(first))
    def _():
        pl.semaphore_signal(barrier, inc=1, device_id={"domain": domain - 1}, device_id_type=MESH)

    @pl.when(jnp.logical_not(last))
    def _():
        pl.semaphore_signal(barrier, inc=1, device_id={"domain": domain + 1}, device_id_type=MESH)

    lax.fori_loop(1, members, greet, 0)
    for load in loads:
        load.wait()

    for p in range(parts):
        halo_out[0, 2 * p : 2 * p + 2] = x[p, 0:2]
        halo_out[1, 2 * p : 2 * p + 2] = x[p, rows - 2 : rows]
    for f in range(fields):
        at = 2 * (parts + f)
        halo_out[0, at : at + 2] = flux[f, 0:2]
        halo_out[1, at : at + 2] = flux[f, rows - 2 : rows]
    masks(land[SUB : SUB + rows].astype(jnp.float32), table)
    step(x, mid, table, flux, diffusivity, mixing)
    step(mid, fore, table, flux, diffusivity, mixing)

    def pack(tile):
        for p in range(parts):
            k = (p % per_chunk) * tile_rows
            sent[p // per_chunk, tile, k : k + tile_rows] = fore[
                p, tile * tile_rows : (tile + 1) * tile_rows
            ]

    for tile in range(1, members - 1):
        pack(tile)

    greeted = members - 1 + (1 - first.astype(jnp.int32)) + (1 - last.astype(jnp.int32))
    pl.semaphore_wait(barrier, greeted)

    to_upper = pltpu.make_async_remote_copy(
        halo_out.at[0], halo_in.at[1], halo_send.at[0], halo_recv.at[1],
        device_id={"domain": jnp.maximum(domain - 1, 0)}, device_id_type=MESH,
    )
    to_lower = pltpu.make_async_remote_copy(
        halo_out.at[1], halo_in.at[0], halo_send.at[1], halo_recv.at[0],
        device_id={"domain": jnp.minimum(domain + 1, domains - 1)}, device_id_type=MESH,
    )

    @pl.when(jnp.logical_not(first))
    def _():
        to_upper.start()

    @pl.when(jnp.logical_not(last))
    def _():
        to_lower.start()

    def send(chunk, peer):
        pltpu.make_async_remote_copy(
            sent.at[chunk, peer], got.at[chunk, me], fore_send, fore_recv.at[chunk],
            device_id={"member": peer}, device_id_type=MESH,
        ).start()

    early = (chunks + 1) // 2

    def send_all(low, high, wanted):
        def one(i, carry):
            chunk = low + i // (members - 1)
            peer = lax.rem(me + 1 + lax.rem(i, members - 1), members)

            @pl.when(wanted(peer))
            def _():
                send(chunk, peer)

            return carry

        lax.fori_loop(0, (high - low) * (members - 1), one, 0)

    send_all(0, early, lambda t: jnp.logical_and(t > 0, t < members - 1))

    @pl.when(first)
    def _():
        halo_in[0] = jnp.zeros_like(halo_in[0])

    @pl.when(last)
    def _():
        halo_in[1] = jnp.zeros_like(halo_in[1])

    half = SUB
    land_f = land[...].astype(jnp.float32)
    upper = land_f[SUB - 2 : SUB] * (1.0 - first.astype(jnp.float32))
    lower = land_f[SUB + rows : SUB + rows + 2] * (1.0 - last.astype(jnp.float32))
    masks(
        jnp.concatenate(
            [upper, land_f[SUB : SUB + 6], land_f[SUB + rows - 6 : SUB + rows], lower], axis=0
        ),
        edge_table,
    )
    for p in range(parts):
        edge[p, 2:half] = x[p, 0:6]
        edge[p, half : half + 6] = x[p, rows - 6 : rows]
    for f in range(fields):
        edge_flux[f, 2:half] = flux[f, 0:6]
        edge_flux[f, half : half + 6] = flux[f, rows - 6 : rows]

    @pl.when(jnp.logical_not(first))
    def _():
        to_lower.wait_recv()

    @pl.when(jnp.logical_not(last))
    def _():
        to_upper.wait_recv()

    for p in range(parts):
        edge[p, 0:2] = halo_in[0, 2 * p : 2 * p + 2]
        edge[p, half + 6 : half + 8] = halo_in[1, 2 * p : 2 * p + 2]
    for f in range(fields):
        at = 2 * (parts + f)
        edge_flux[f, 0:2] = halo_in[0, at : at + 2]
        edge_flux[f, half + 6 : half + 8] = halo_in[1, at : at + 2]
    step(edge, edge_mid, edge_table, edge_flux, diffusivity, mixing)
    step(edge_mid, edge, edge_table, edge_flux, diffusivity, mixing)
    for p in range(parts):
        fore[p, 0:2] = edge[p, 2:4]
        fore[p, rows - 2 : rows] = edge[p, half + 4 : half + 6]
    pack(0)
    pack(members - 1)
    send_all(0, early, lambda t: jnp.logical_or(t == 0, t == members - 1))
    for c in range(chunks):
        got[c, me] = sent[c, me]

    slots = index.shape[1]
    rank = lax.broadcasted_iota(jnp.int32, (1, slots), 1)
    active = (rank < count[0, me]).astype(jnp.float32)
    weight = active / error[pl.ds(me, 1), :]
    pair = jnp.concatenate(
        [weight, weight * value[pl.ds(me, 1), :], jnp.zeros((SUB - 2, slots), jnp.float32)], axis=0
    )
    where = index[pl.ds(me, 1), :]
    cells = []
    for r in range(tile_rows):
        cell = lax.broadcasted_iota(jnp.int32, (width, slots), 0) + r * width
        hit = (cell == where).astype(jnp.float32)
        cells.append(
            lax.dot_general(pair, hit, NT, precision=EXACT, preferred_element_type=jnp.float32)
        )
    rhs[...] = jnp.zeros_like(rhs)
    for k in range(SUB):
        at = SUB + me * tile_rows + k % tile_rows
        tile_mask[k : k + 1] = land[pl.ds(at, 1), :].astype(jnp.float32)

    def arrived(buffer, semaphore):
        pltpu.make_async_copy(buffer, buffer, semaphore).wait()

    arrived(got.at[0, pl.ds(0, members - 1)], fore_recv.at[0])

    sums = None
    for r in range(tile_rows):
        surface = jnp.concatenate([got[0, m, r : r + 1] for m in range(members)], axis=0)
        average = jnp.mean(surface, axis=0, keepdims=True)
        anomaly = surface - average
        cell_weight = cells[r][0:1]
        rhs[0:members] = anomaly * cell_weight
        rhs[members : members + 1] = cells[r][1:2] - cell_weight * average
        partial = lax.dot_general(
            anomaly, rhs[...], NT, precision=EXACT, preferred_element_type=jnp.float32
        )
        sums = partial if sums is None else sums + partial
    sums_out[...] = sums
    sums_in[me] = sums

    def send_sums(i, carry):
        peer = lax.rem(me + i, members)
        pltpu.make_async_remote_copy(
            sums_out, sums_in.at[me], sums_send, sums_recv,
            device_id={"member": peer}, device_id_type=MESH,
        ).start()
        return carry

    lax.fori_loop(1, members, send_sums, 0)
    send_all(early, chunks, lambda t: t >= 0)
    arrived(sums_in.at[pl.ds(0, members - 1)], sums_recv)

    total = sums_in[0]
    for m in range(1, members):
        total += sums_in[m]
    row = lax.broadcasted_iota(jnp.int32, total.shape, 0)
    lane = lax.broadcasted_iota(jnp.int32, total.shape, 1)
    system = total + jnp.where(lane == row, members - 1.0, 0.0)
    system = jnp.where(lane > members, jnp.where(lane == row + members + 1, 1.0, 0.0), system)

    def eliminate(k, a):
        pivot_row = jnp.sum(jnp.where(row == k, a, 0.0), axis=0, keepdims=True)
        column = jnp.sum(jnp.where(lane == k, a, 0.0), axis=1, keepdims=True)
        pivot = jnp.sum(jnp.where(lane[0:1] == k, pivot_row, 0.0), axis=1, keepdims=True)
        root = jnp.sqrt(pivot)
        return jnp.where(
            row == k, a / root, jnp.where(row > k, a - (column / pivot) * pivot_row, a)
        )

    system = lax.fori_loop(0, members, eliminate, system)
    inner = jnp.sum(jnp.where(lane == members, system, 0.0), axis=1, keepdims=True)
    mean_weight = jnp.sum(system * inner, axis=0, keepdims=True)
    weights = mean_weight + jnp.sqrt(jnp.float32(members - 1.0)) * system
    own = jnp.logical_and(lane > members, lane <= 2 * members)
    weights = jnp.where(own, weights, 0.0)
    weights = weights - jnp.sum(weights, axis=1, keepdims=True) / members + 1.0 / members
    for j in range(members):
        column = jnp.sum(jnp.where(lane == members + 1 + j, weights, 0.0), axis=1, keepdims=True)
        spread[j] = jnp.broadcast_to(column, (members, LANES))

    for c in range(chunks):
        if c > 0:
            arrived(got.at[c, pl.ds(0, members - 1)], fore_recv.at[c])

        def update(m, carry):
            for q in range(width // LANES):
                part = pl.ds(q * LANES, LANES)
                acc = None
                for j in range(members):
                    term = spread[j, pl.ds(m, 1), :] * got[c, j, :, part]
                    acc = term if acc is None else acc + term
                reply[c, m, :, part] = jnp.where(
                    tile_mask[:, part] > 0, acc, got[c, m, :, part]
                )
            return carry

        lax.fori_loop(0, members, update, 0)

        def send_reply(i, carry):
            peer = lax.rem(me + i, members)
            pltpu.make_async_remote_copy(
                reply.at[c, peer], out.at[c, me], reply_send, reply_recv,
                device_id={"member": peer}, device_id_type=MESH,
            ).start()
            return carry

        lax.fori_loop(1, members, send_reply, 0)
        out[c, me] = reply[c, me]

    blocks = (slice(None), pl.ds(0, members - 1))
    arrived(out.at[blocks], reply_recv)
    arrived(sent.at[blocks], fore_send)
    arrived(reply.at[blocks], reply_send)
    arrived(sums_in.at[pl.ds(0, members - 1)], sums_send)

    @pl.when(jnp.logical_not(first))
    def _():
        to_upper.wait_send()

    @pl.when(jnp.logical_not(last))
    def _():
        to_lower.wait_send()


def shards(
    starting_tracer_fields, surface_exchange_inputs, diffusivity, mixing, land_mask,
    obs_index, obs_count, obs_value, obs_error,
):
    members = lax.axis_size("member")
    domains = lax.axis_size("domain")
    _, fields, levels, rows, width = starting_tracer_fields.shape
    parts = fields * levels
    tile_rows = rows // members
    chunks = parts * tile_rows // SUB
    sums_width = pl.cdiv(2 * members + 1, LANES) * LANES
    halo_rows = pl.cdiv(2 * (parts + fields), SUB) * SUB
    tiles, slots = obs_index.shape[1:]
    f32, i32 = jnp.float32, jnp.int32
    vmem = pltpu.VMEM
    dma = pltpu.SemaphoreType.DMA
    window = 2 * SUB
    blocks = (chunks, members, SUB, width)
    anywhere = pl.BlockSpec(memory_space=pl.ANY)
    scalars = pl.BlockSpec(memory_space=pltpu.SMEM)
    result = pl.pallas_call(
        functools.partial(body, members, domains),
        out_shape=jax.ShapeDtypeStruct(blocks, f32),
        in_specs=[anywhere] * 6 + [scalars] * 3,
        out_specs=pl.BlockSpec(memory_space=pltpu.VMEM),
        scratch_shapes=[
            vmem((parts, rows, width), f32),
            vmem((fields, rows, width), f32),
            vmem((rows + 2 * SUB, width), i32),
            vmem((tiles, slots), i32),
            vmem((tiles, slots), f32),
            vmem((tiles, slots), f32),
            vmem((parts, rows, width), f32),
            vmem((parts, rows, width), f32),
            vmem((5, rows, width), f32),
            vmem((2, halo_rows, width), f32),
            vmem((2, halo_rows, width), f32),
            vmem((parts, window, width), f32),
            vmem((parts, window, width), f32),
            vmem((fields, window, width), f32),
            vmem((5, window, width), f32),
            vmem(blocks, f32),
            vmem(blocks, f32),
            vmem((sums_width, width), f32),
            vmem((members, sums_width), f32),
            vmem((members, members, sums_width), f32),
            vmem((members, members, LANES), f32),
            vmem((SUB, width), f32),
            vmem(blocks, f32),
            dma((8,)),
            dma((2,)),
            dma((2,)),
            dma,
            dma((chunks,)),
            dma,
            dma,
            dma,
            dma,
        ],
        compiler_params=pltpu.CompilerParams(
            collective_id=0, has_side_effects=True, vmem_limit_bytes=56 * 1024 * 1024
        ),
    )(
        starting_tracer_fields.reshape(parts, rows, width),
        surface_exchange_inputs.reshape(fields, rows, width),
        land_mask,
        obs_index.reshape(tiles, slots),
        obs_value.reshape(tiles, slots),
        obs_error.reshape(tiles, slots),
        obs_count.reshape(1, tiles),
        diffusivity,
        mixing,
    )
    result = result.reshape(chunks, members, SUB // tile_rows, tile_rows, width)
    result = jnp.swapaxes(result, 1, 2)
    return result.reshape(starting_tracer_fields.shape)


def solution(mesh):
    placed = (
        P("member", None, None, "domain", None),
        P("member", None, "domain", None),
        P(),
        P(),
        P(),
        P("domain", None, None),
        P("domain", None),
        P("domain", None, None),
        P("domain", None, None),
    )
    return jax.shard_map(
        shards,
        mesh=mesh,
        in_specs=placed,
        out_specs=P("member", None, None, "domain", None),
        check_vma=False,
    )
```

```python
import functools

import jax
import jax.numpy as jnp
from jax import lax
from jax.experimental import pallas as pl
from jax.experimental.pallas import tpu as pltpu
from jax.sharding import PartitionSpec as P

STEPS = 2
SUB = 8
LANES = 128
EXACT = lax.Precision.HIGHEST
MESH = pl.DeviceIdType.MESH
NT = (((1,), (1,)), ((), ()))


def masks(mask, table):
    rows, width = mask.shape
    table[0] = mask
    table[1] = pltpu.roll(mask, rows - 1, 0)
    table[2] = pltpu.roll(mask, 1, 0)
    table[3] = pltpu.roll(mask, width - 1, 1)
    table[4] = pltpu.roll(mask, 1, 1)


def step(source, target, table, flux, diffusivity, mixing):
    fields, levels = diffusivity.shape
    rows, width = source.shape[1:]

    def one(f, carry):
        above = None
        for l in range(levels):
            x = source[f * levels + l]
            lateral = table[1] * (pltpu.roll(x, rows - 1, 0) - x)
            lateral += table[2] * (pltpu.roll(x, 1, 0) - x)
            lateral += table[3] * (pltpu.roll(x, width - 1, 1) - x)
            lateral += table[4] * (pltpu.roll(x, 1, 1) - x)
            change = diffusivity[f, l] * lateral
            if l < levels - 1:
                down = mixing[f, l] * (source[f * levels + l + 1] - x)
                change += down
            if l > 0:
                change -= above
            else:
                change += flux[f]
            above = down
            target[f * levels + l] = x + table[0] * change
        return carry

    lax.fori_loop(0, fields, one, 0)


def body(
    members, domains, x_hbm, flux_hbm, mask_hbm, index_hbm, value_hbm, error_hbm,
    count, diffusivity, mixing, out,
    x, flux, land, index, value, error, mid, fore, table,
    halo_out, halo_in, edge, edge_mid, edge_flux, edge_table,
    sent, got, rhs, sums_out, sums_in, spread, tile_mask, reply, back,
    load_sem, halo_send, halo_recv, fore_send, fore_recv,
    sums_send, sums_recv, reply_send, reply_recv,
):
    me = lax.axis_index("member")
    domain = lax.axis_index("domain")
    parts, rows, width = x.shape
    fields = flux.shape[0]
    chunks = got.shape[0]
    tile_rows = rows // members
    per_chunk = SUB // tile_rows
    lat = mask_hbm.shape[0]
    first = domain == 0
    last = domain == domains - 1
    start_row = pl.multiple_of(domain * rows, SUB)
    above_row = pl.multiple_of(jnp.maximum(domain * rows - SUB, 0), SUB)
    below_row = pl.multiple_of(jnp.minimum(domain * rows + rows, lat - SUB), SUB)

    loads = [
        pltpu.make_async_copy(a, b, load_sem.at[i])
        for i, (a, b) in enumerate((
            (x_hbm, x),
            (flux_hbm, flux),
            (mask_hbm.at[pl.ds(above_row, SUB)], land.at[pl.ds(0, SUB)]),
            (mask_hbm.at[pl.ds(start_row, rows)], land.at[pl.ds(SUB, rows)]),
            (mask_hbm.at[pl.ds(below_row, SUB)], land.at[pl.ds(SUB + rows, SUB)]),
            (index_hbm, index),
            (value_hbm, value),
            (error_hbm, error),
        ))
    ]
    for load in loads:
        load.start()

    barrier = pltpu.get_barrier_semaphore()

    def greet(i, carry):
        peer = lax.rem(me + i, members)
        pl.semaphore_signal(barrier, inc=1, device_id={"member": peer}, device_id_type=MESH)
        return carry

    @pl.when(jnp.logical_not(first))
    def _():
        pl.semaphore_signal(barrier, inc=1, device_id={"domain": domain - 1}, device_id_type=MESH)

    @pl.when(jnp.logical_not(last))
    def _():
        pl.semaphore_signal(barrier, inc=1, device_id={"domain": domain + 1}, device_id_type=MESH)

    lax.fori_loop(1, members, greet, 0)
    for load in loads:
        load.wait()

    for p in range(parts):
        halo_out[0, 2 * p : 2 * p + 2] = x[p, 0:2]
        halo_out[1, 2 * p : 2 * p + 2] = x[p, rows - 2 : rows]
    for f in range(fields):
        at = 2 * (parts + f)
        halo_out[0, at : at + 2] = flux[f, 0:2]
        halo_out[1, at : at + 2] = flux[f, rows - 2 : rows]
    masks(land[SUB : SUB + rows].astype(jnp.float32), table)
    step(x, mid, table, flux, diffusivity, mixing)
    step(mid, fore, table, flux, diffusivity, mixing)

    def pack(tile):
        for p in range(parts):
            k = (p % per_chunk) * tile_rows
            sent[p // per_chunk, tile, k : k + tile_rows] = fore[
                p, tile * tile_rows : (tile + 1) * tile_rows
            ]

    for tile in range(1, members - 1):
        pack(tile)

    greeted = members - 1 + (1 - first.astype(jnp.int32)) + (1 - last.astype(jnp.int32))
    pl.semaphore_wait(barrier, greeted)

    to_upper = pltpu.make_async_remote_copy(
        halo_out.at[0], halo_in.at[1], halo_send.at[0], halo_recv.at[1],
        device_id={"domain": jnp.maximum(domain - 1, 0)}, device_id_type=MESH,
    )
    to_lower = pltpu.make_async_remote_copy(
        halo_out.at[1], halo_in.at[0], halo_send.at[1], halo_recv.at[0],
        device_id={"domain": jnp.minimum(domain + 1, domains - 1)}, device_id_type=MESH,
    )

    @pl.when(jnp.logical_not(first))
    def _():
        to_upper.start()

    @pl.when(jnp.logical_not(last))
    def _():
        to_lower.start()

    def send(chunk, peer):
        pltpu.make_async_remote_copy(
            sent.at[chunk, peer], got.at[chunk, me], fore_send, fore_recv.at[chunk],
            device_id={"member": peer}, device_id_type=MESH,
        ).start()

    early = (chunks + 1) // 2

    def send_all(low, high, wanted):
        def one(i, carry):
            chunk = low + i // (members - 1)
            peer = lax.rem(me + 1 + lax.rem(i, members - 1), members)

            @pl.when(wanted(peer))
            def _():
                send(chunk, peer)

            return carry

        lax.fori_loop(0, (high - low) * (members - 1), one, 0)

    send_all(0, early, lambda t: jnp.logical_and(t > 0, t < members - 1))

    @pl.when(first)
    def _():
        halo_in[0] = jnp.zeros_like(halo_in[0])

    @pl.when(last)
    def _():
        halo_in[1] = jnp.zeros_like(halo_in[1])

    half = SUB
    land_f = land[...].astype(jnp.float32)
    upper = land_f[SUB - 2 : SUB] * (1.0 - first.astype(jnp.float32))
    lower = land_f[SUB + rows : SUB + rows + 2] * (1.0 - last.astype(jnp.float32))
    masks(
        jnp.concatenate(
            [upper, land_f[SUB : SUB + 6], land_f[SUB + rows - 6 : SUB + rows], lower], axis=0
        ),
        edge_table,
    )
    for p in range(parts):
        edge[p, 2:half] = x[p, 0:6]
        edge[p, half : half + 6] = x[p, rows - 6 : rows]
    for f in range(fields):
        edge_flux[f, 2:half] = flux[f, 0:6]
        edge_flux[f, half : half + 6] = flux[f, rows - 6 : rows]

    @pl.when(jnp.logical_not(first))
    def _():
        to_lower.wait_recv()

    @pl.when(jnp.logical_not(last))
    def _():
        to_upper.wait_recv()

    for p in range(parts):
        edge[p, 0:2] = halo_in[0, 2 * p : 2 * p + 2]
        edge[p, half + 6 : half + 8] = halo_in[1, 2 * p : 2 * p + 2]
    for f in range(fields):
        at = 2 * (parts + f)
        edge_flux[f, 0:2] = halo_in[0, at : at + 2]
        edge_flux[f, half + 6 : half + 8] = halo_in[1, at : at + 2]
    step(edge, edge_mid, edge_table, edge_flux, diffusivity, mixing)
    step(edge_mid, edge, edge_table, edge_flux, diffusivity, mixing)
    for p in range(parts):
        fore[p, 0:2] = edge[p, 2:4]
        fore[p, rows - 2 : rows] = edge[p, half + 4 : half + 6]
    pack(0)
    pack(members - 1)
    send_all(0, early, lambda t: jnp.logical_or(t == 0, t == members - 1))
    for c in range(chunks):
        got[c, me] = sent[c, me]

    slots = index.shape[1]
    rank = lax.broadcasted_iota(jnp.int32, (1, slots), 1)
    active = (rank < count[0, me]).astype(jnp.float32)
    weight = active / error[pl.ds(me, 1), :]
    pair = jnp.concatenate(
        [weight, weight * value[pl.ds(me, 1), :], jnp.zeros((SUB - 2, slots), jnp.float32)], axis=0
    )
    where = index[pl.ds(me, 1), :]
    cells = []
    for r in range(tile_rows):
        cell = lax.broadcasted_iota(jnp.int32, (width, slots), 0) + r * width
        hit = (cell == where).astype(jnp.float32)
        cells.append(
            lax.dot_general(pair, hit, NT, precision=EXACT, preferred_element_type=jnp.float32)
        )
    rhs[...] = jnp.zeros_like(rhs)
    for k in range(SUB):
        at = SUB + me * tile_rows + k % tile_rows
        tile_mask[k : k + 1] = land[pl.ds(at, 1), :].astype(jnp.float32)

    def arrived(buffer, semaphore):
        pltpu.make_async_copy(buffer, buffer, semaphore).wait()

    arrived(got.at[0, pl.ds(0, members - 1)], fore_recv.at[0])

    sums = None
    for r in range(tile_rows):
        surface = jnp.concatenate([got[0, m, r : r + 1] for m in range(members)], axis=0)
        average = jnp.mean(surface, axis=0, keepdims=True)
        anomaly = surface - average
        cell_weight = cells[r][0:1]
        rhs[0:members] = anomaly * cell_weight
        rhs[members : members + 1] = cells[r][1:2] - cell_weight * average
        partial = lax.dot_general(
            anomaly, rhs[...], NT, precision=EXACT, preferred_element_type=jnp.float32
        )
        sums = partial if sums is None else sums + partial
    sums_out[...] = sums
    sums_in[me] = sums

    def send_sums(i, carry):
        peer = lax.rem(me + i, members)
        pltpu.make_async_remote_copy(
            sums_out, sums_in.at[me], sums_send, sums_recv,
            device_id={"member": peer}, device_id_type=MESH,
        ).start()
        return carry

    lax.fori_loop(1, members, send_sums, 0)
    send_all(early, chunks, lambda t: t >= 0)
    arrived(sums_in.at[pl.ds(0, members - 1)], sums_recv)

    total = sums_in[0]
    for m in range(1, members):
        total += sums_in[m]
    row = lax.broadcasted_iota(jnp.int32, total.shape, 0)
    lane = lax.broadcasted_iota(jnp.int32, total.shape, 1)
    system = total + jnp.where(lane == row, members - 1.0, 0.0)
    system = jnp.where(lane > members, jnp.where(lane == row + members + 1, 1.0, 0.0), system)

    def eliminate(k, a):
        pivot_row = jnp.sum(jnp.where(row == k, a, 0.0), axis=0, keepdims=True)
        column = jnp.sum(jnp.where(lane == k, a, 0.0), axis=1, keepdims=True)
        pivot = jnp.sum(jnp.where(lane[0:1] == k, pivot_row, 0.0), axis=1, keepdims=True)
        root = jnp.sqrt(pivot)
        return jnp.where(
            row == k, a / root, jnp.where(row > k, a - (column / pivot) * pivot_row, a)
        )

    system = lax.fori_loop(0, members, eliminate, system)
    inner = jnp.sum(jnp.where(lane == members, system, 0.0), axis=1, keepdims=True)
    mean_weight = jnp.sum(system * inner, axis=0, keepdims=True)
    weights = mean_weight + jnp.sqrt(jnp.float32(members - 1.0)) * system
    own = jnp.logical_and(lane > members, lane <= 2 * members)
    weights = jnp.where(own, weights, 0.0)
    weights = weights - jnp.sum(weights, axis=1, keepdims=True) / members + 1.0 / members
    for j in range(members):
        column = jnp.sum(jnp.where(lane == members + 1 + j, weights, 0.0), axis=1, keepdims=True)
        spread[j] = jnp.broadcast_to(column, (members, LANES))

    for c in range(chunks):
        if c > 0:
            arrived(got.at[c, pl.ds(0, members - 1)], fore_recv.at[c])

        def update(m, carry):
            for q in range(width // LANES):
                part = pl.ds(q * LANES, LANES)
                acc = None
                for j in range(members):
                    term = spread[j, pl.ds(m, 1), :] * got[c, j, :, part]
                    acc = term if acc is None else acc + term
                reply[c, m, :, part] = jnp.where(
                    tile_mask[:, part] > 0, acc, got[c, m, :, part]
                )
            return carry

        lax.fori_loop(0, members, update, 0)

        def send_reply(i, carry):
            peer = lax.rem(me + i, members)
            pltpu.make_async_remote_copy(
                reply.at[c, peer], back.at[c, me], reply_send, reply_recv.at[c],
                device_id={"member": peer}, device_id_type=MESH,
            ).start()
            return carry

        lax.fori_loop(1, members, send_reply, 0)
        back[c, me] = reply[c, me]

    for c in range(chunks):
        arrived(back.at[c, pl.ds(0, members - 1)], reply_recv.at[c])
        for k in range(per_chunk):
            for tile in range(members):
                out[c * per_chunk + k, tile * tile_rows : (tile + 1) * tile_rows] = back[
                    c, tile, k * tile_rows : (k + 1) * tile_rows
                ]

    blocks = (slice(None), pl.ds(0, members - 1))
    arrived(sent.at[blocks], fore_send)
    arrived(reply.at[blocks], reply_send)
    arrived(sums_in.at[pl.ds(0, members - 1)], sums_send)

    @pl.when(jnp.logical_not(first))
    def _():
        to_upper.wait_send()

    @pl.when(jnp.logical_not(last))
    def _():
        to_lower.wait_send()


def shards(
    starting_tracer_fields, surface_exchange_inputs, diffusivity, mixing, land_mask,
    obs_index, obs_count, obs_value, obs_error,
):
    members = lax.axis_size("member")
    domains = lax.axis_size("domain")
    _, fields, levels, rows, width = starting_tracer_fields.shape
    parts = fields * levels
    tile_rows = rows // members
    chunks = parts * tile_rows // SUB
    sums_width = pl.cdiv(2 * members + 1, LANES) * LANES
    halo_rows = pl.cdiv(2 * (parts + fields), SUB) * SUB
    tiles, slots = obs_index.shape[1:]
    f32, i32 = jnp.float32, jnp.int32
    vmem = pltpu.VMEM
    dma = pltpu.SemaphoreType.DMA
    window = 2 * SUB
    blocks = (chunks, members, SUB, width)
    anywhere = pl.BlockSpec(memory_space=pl.ANY)
    scalars = pl.BlockSpec(memory_space=pltpu.SMEM)
    result = pl.pallas_call(
        functools.partial(body, members, domains),
        out_shape=pltpu.VMEM((parts, rows, width), f32),
        in_specs=[anywhere] * 6 + [scalars] * 3,
        out_specs=pl.BlockSpec(memory_space=pltpu.VMEM),
        scratch_shapes=[
            vmem((parts, rows, width), f32),
            vmem((fields, rows, width), f32),
            vmem((rows + 2 * SUB, width), i32),
            vmem((tiles, slots), i32),
            vmem((tiles, slots), f32),
            vmem((tiles, slots), f32),
            vmem((parts, rows, width), f32),
            vmem((parts, rows, width), f32),
            vmem((5, rows, width), f32),
            vmem((2, halo_rows, width), f32),
            vmem((2, halo_rows, width), f32),
            vmem((parts, window, width), f32),
            vmem((parts, window, width), f32),
            vmem((fields, window, width), f32),
            vmem((5, window, width), f32),
            vmem(blocks, f32),
            vmem(blocks, f32),
            vmem((sums_width, width), f32),
            vmem((members, sums_width), f32),
            vmem((members, members, sums_width), f32),
            vmem((members, members, LANES), f32),
            vmem((SUB, width), f32),
            vmem(blocks, f32),
            vmem(blocks, f32),
            dma((8,)),
            dma((2,)),
            dma((2,)),
            dma,
            dma((chunks,)),
            dma,
            dma,
            dma,
            dma((chunks,)),
        ],
        compiler_params=pltpu.CompilerParams(
            collective_id=0, has_side_effects=True, vmem_limit_bytes=56 * 1024 * 1024
        ),
    )(
        starting_tracer_fields.reshape(parts, rows, width),
        surface_exchange_inputs.reshape(fields, rows, width),
        land_mask,
        obs_index.reshape(tiles, slots),
        obs_value.reshape(tiles, slots),
        obs_error.reshape(tiles, slots),
        obs_count.reshape(1, tiles),
        diffusivity,
        mixing,
    )
    return result.reshape(starting_tracer_fields.shape)


def solution(mesh):
    placed = (
        P("member", None, None, "domain", None),
        P("member", None, "domain", None),
        P(),
        P(),
        P(),
        P("domain", None, None),
        P("domain", None),
        P("domain", None, None),
        P("domain", None, None),
    )
    return jax.shard_map(
        shards,
        mesh=mesh,
        in_specs=placed,
        out_specs=P("member", None, None, "domain", None),
        check_vma=False,
    )
```

```python
import functools

import jax
import jax.numpy as jnp
from jax import lax
from jax.experimental import pallas as pl
from jax.experimental.pallas import tpu as pltpu
from jax.sharding import PartitionSpec as P

STEPS = 2
SUB = 8
LANES = 128
EXACT = lax.Precision.HIGHEST
MESH = pl.DeviceIdType.MESH
NT = (((1,), (1,)), ((), ()))


def masks(mask, table):
    rows, width = mask.shape
    table[0] = mask
    table[1] = pltpu.roll(mask, rows - 1, 0)
    table[2] = pltpu.roll(mask, 1, 0)
    table[3] = pltpu.roll(mask, width - 1, 1)
    table[4] = pltpu.roll(mask, 1, 1)


def step(f, source, target, table, flux, diffusivity, mixing):
    levels = diffusivity.shape[1]
    rows, width = source.shape[1:]
    above = None
    for l in range(levels):
        x = source[f * levels + l]
        lateral = table[1] * (pltpu.roll(x, rows - 1, 0) - x)
        lateral += table[2] * (pltpu.roll(x, 1, 0) - x)
        lateral += table[3] * (pltpu.roll(x, width - 1, 1) - x)
        lateral += table[4] * (pltpu.roll(x, 1, 1) - x)
        change = diffusivity[f, l] * lateral
        if l < levels - 1:
            down = mixing[f, l] * (source[f * levels + l + 1] - x)
            change += down
        if l > 0:
            change -= above
        else:
            change += flux[f]
        above = down
        target[f * levels + l] = x + table[0] * change


def body(
    members, domains, x_hbm, flux_hbm, mask_hbm, index_hbm, value_hbm, error_hbm,
    count, diffusivity, mixing, out,
    x, flux, land, index, value, error, mid, fore, table,
    halo_out, halo_in, edge, edge_mid, edge_flux, edge_table,
    sent, got, rhs, sums_out, sums_in, spread, tile_mask, reply, back,
    load_sem, halo_send, halo_recv, fore_send, fore_recv,
    sums_send, sums_recv, reply_send, reply_recv,
):
    me = lax.axis_index("member")
    domain = lax.axis_index("domain")
    parts, rows, width = x.shape
    fields, levels = diffusivity.shape
    chunks = got.shape[0]
    tile_rows = rows // members
    per_chunk = SUB // tile_rows
    lat = mask_hbm.shape[0]
    first = domain == 0
    last = domain == domains - 1
    start_row = pl.multiple_of(domain * rows, SUB)
    above_row = pl.multiple_of(jnp.maximum(domain * rows - SUB, 0), SUB)
    below_row = pl.multiple_of(jnp.minimum(domain * rows + rows, lat - SUB), SUB)

    barrier = pltpu.get_barrier_semaphore()

    def greet(i, carry):
        peer = lax.rem(me + i, members)
        pl.semaphore_signal(barrier, inc=1, device_id={"member": peer}, device_id_type=MESH)
        return carry

    @pl.when(jnp.logical_not(first))
    def _():
        pl.semaphore_signal(barrier, inc=1, device_id={"domain": domain - 1}, device_id_type=MESH)

    @pl.when(jnp.logical_not(last))
    def _():
        pl.semaphore_signal(barrier, inc=1, device_id={"domain": domain + 1}, device_id_type=MESH)

    lax.fori_loop(1, members, greet, 0)

    loads = [
        pltpu.make_async_copy(a, b, load_sem.at[i])
        for i, (a, b) in enumerate((
            (x_hbm, x),
            (flux_hbm, flux),
            (mask_hbm.at[pl.ds(above_row, SUB)], land.at[pl.ds(0, SUB)]),
            (mask_hbm.at[pl.ds(start_row, rows)], land.at[pl.ds(SUB, rows)]),
            (mask_hbm.at[pl.ds(below_row, SUB)], land.at[pl.ds(SUB + rows, SUB)]),
            (index_hbm, index),
            (value_hbm, value),
            (error_hbm, error),
        ))
    ]
    for load in loads:
        load.start()

    for load in loads:
        load.wait()

    for f in range(fields):
        for l in range(levels + 1):
            line = x.at[f * levels + l] if l < levels else flux.at[f]
            halo_out[0, f, 2 * l : 2 * l + 2] = line[0:2]
            halo_out[1, f, 2 * l : 2 * l + 2] = line[rows - 2 : rows]
    masks(land[SUB : SUB + rows].astype(jnp.float32), table)

    def pack(tile, f):
        for p in range(f * levels, (f + 1) * levels):
            k = (p % per_chunk) * tile_rows
            sent[p // per_chunk, tile, k : k + tile_rows] = fore[
                p, tile * tile_rows : (tile + 1) * tile_rows
            ]

    def interior(f):
        step(f, x, mid, table, flux, diffusivity, mixing)
        step(f, mid, fore, table, flux, diffusivity, mixing)
        for tile in range(1, members - 1):
            pack(tile, f)

    interior(0)
    greeted = members - 1 + (1 - first.astype(jnp.int32)) + (1 - last.astype(jnp.int32))
    pl.semaphore_wait(barrier, greeted)

    to_upper = [
        pltpu.make_async_remote_copy(
            halo_out.at[0, f], halo_in.at[1, f], halo_send.at[0, f], halo_recv.at[1, f],
            device_id={"domain": jnp.maximum(domain - 1, 0)}, device_id_type=MESH,
        )
        for f in range(fields)
    ]
    to_lower = [
        pltpu.make_async_remote_copy(
            halo_out.at[1, f], halo_in.at[0, f], halo_send.at[1, f], halo_recv.at[0, f],
            device_id={"domain": jnp.minimum(domain + 1, domains - 1)}, device_id_type=MESH,
        )
        for f in range(fields)
    ]

    @pl.when(jnp.logical_not(first))
    def _():
        for copy in to_upper:
            copy.start()

    @pl.when(jnp.logical_not(last))
    def _():
        for copy in to_lower:
            copy.start()

    def send(chunk, peer):
        pltpu.make_async_remote_copy(
            sent.at[chunk, peer], got.at[chunk, me], fore_send, fore_recv.at[chunk],
            device_id={"member": peer}, device_id_type=MESH,
        ).start()

    early = chunks // fields

    def send_all(low, high, wanted):
        def one(i, carry):
            chunk = i // (members - 1)
            peer = lax.rem(me + 1 + lax.rem(i, members - 1), members)

            @pl.when(wanted(peer))
            def _():
                send(chunk, peer)

            return carry

        lax.fori_loop(low, high, one, 0)

    turn = members - 1
    ahead = turn
    inner = lambda t: jnp.logical_and(t > 0, t < members - 1)
    outer = lambda t: jnp.logical_or(t == 0, t == members - 1)
    send_all(0, ahead, inner)

    @pl.when(first)
    def _():
        halo_in[0] = jnp.zeros_like(halo_in[0])

    @pl.when(last)
    def _():
        halo_in[1] = jnp.zeros_like(halo_in[1])

    half = SUB
    land_f = land[...].astype(jnp.float32)
    upper = land_f[SUB - 2 : SUB] * (1.0 - first.astype(jnp.float32))
    lower = land_f[SUB + rows : SUB + rows + 2] * (1.0 - last.astype(jnp.float32))
    masks(
        jnp.concatenate(
            [upper, land_f[SUB : SUB + 6], land_f[SUB + rows - 6 : SUB + rows], lower], axis=0
        ),
        edge_table,
    )
    for p in range(parts):
        edge[p, 2:half] = x[p, 0:6]
        edge[p, half : half + 6] = x[p, rows - 6 : rows]
    for f in range(fields):
        edge_flux[f, 2:half] = flux[f, 0:6]
        edge_flux[f, half : half + 6] = flux[f, rows - 6 : rows]

    for f in range(1, fields):
        interior(f)

    for f in range(fields):

        @pl.when(jnp.logical_not(first))
        def _():
            to_lower[f].wait_recv()

        @pl.when(jnp.logical_not(last))
        def _():
            to_upper[f].wait_recv()

        for l in range(levels + 1):
            line = edge.at[f * levels + l] if l < levels else edge_flux.at[f]
            line[0:2] = halo_in[0, f, 2 * l : 2 * l + 2]
            line[half + 6 : half + 8] = halo_in[1, f, 2 * l : 2 * l + 2]
        step(f, edge, edge_mid, edge_table, edge_flux, diffusivity, mixing)
        step(f, edge_mid, edge, edge_table, edge_flux, diffusivity, mixing)
        for p in range(f * levels, (f + 1) * levels):
            fore[p, 0:2] = edge[p, 2:4]
            fore[p, rows - 2 : rows] = edge[p, half + 4 : half + 6]
        pack(0, f)
        pack(members - 1, f)
        if f == 0:
            send_all(0, ahead, outer)
            send_all(ahead, early * turn, lambda t: t >= 0)
    for c in range(chunks):
        got[c, me] = sent[c, me]

    slots = index.shape[1]
    rank = lax.broadcasted_iota(jnp.int32, (1, slots), 1)
    active = (rank < count[0, me]).astype(jnp.float32)
    weight = active / error[pl.ds(me, 1), :]
    pair = jnp.concatenate(
        [weight, weight * value[pl.ds(me, 1), :], jnp.zeros((SUB - 2, slots), jnp.float32)], axis=0
    )
    where = index[pl.ds(me, 1), :]
    cells = []
    for r in range(tile_rows):
        cell = lax.broadcasted_iota(jnp.int32, (width, slots), 0) + r * width
        hit = (cell == where).astype(jnp.float32)
        cells.append(
            lax.dot_general(pair, hit, NT, precision=EXACT, preferred_element_type=jnp.float32)
        )
    rhs[...] = jnp.zeros_like(rhs)
    for k in range(SUB):
        at = SUB + me * tile_rows + k % tile_rows
        tile_mask[k : k + 1] = land[pl.ds(at, 1), :].astype(jnp.float32)

    def arrived(buffer, semaphore):
        pltpu.make_async_copy(buffer, buffer, semaphore).wait()

    arrived(got.at[0, pl.ds(0, members - 1)], fore_recv.at[0])

    sums = None
    for r in range(tile_rows):
        surface = jnp.concatenate([got[0, m, r : r + 1] for m in range(members)], axis=0)
        average = jnp.mean(surface, axis=0, keepdims=True)
        anomaly = surface - average
        cell_weight = cells[r][0:1]
        rhs[0:members] = anomaly * cell_weight
        rhs[members : members + 1] = cells[r][1:2] - cell_weight * average
        partial = lax.dot_general(
            anomaly, rhs[...], NT, precision=EXACT, preferred_element_type=jnp.float32
        )
        sums = partial if sums is None else sums + partial
    sums_out[...] = sums
    sums_in[me] = sums

    def send_sums(i, carry):
        peer = lax.rem(me + i, members)
        pltpu.make_async_remote_copy(
            sums_out, sums_in.at[me], sums_send, sums_recv,
            device_id={"member": peer}, device_id_type=MESH,
        ).start()
        return carry

    lax.fori_loop(1, members, send_sums, 0)
    send_all(early * turn, chunks * turn, lambda t: t >= 0)
    arrived(sums_in.at[pl.ds(0, members - 1)], sums_recv)

    total = sums_in[0]
    for m in range(1, members):
        total += sums_in[m]
    row = lax.broadcasted_iota(jnp.int32, total.shape, 0)
    lane = lax.broadcasted_iota(jnp.int32, total.shape, 1)
    system = total + jnp.where(lane == row, members - 1.0, 0.0)
    system = jnp.where(lane > members, jnp.where(lane == row + members + 1, 1.0, 0.0), system)

    def eliminate(k, a):
        pivot_row = jnp.sum(jnp.where(row == k, a, 0.0), axis=0, keepdims=True)
        column = jnp.sum(jnp.where(lane == k, a, 0.0), axis=1, keepdims=True)
        pivot = jnp.sum(jnp.where(lane[0:1] == k, pivot_row, 0.0), axis=1, keepdims=True)
        root = jnp.sqrt(pivot)
        return jnp.where(
            row == k, a / root, jnp.where(row > k, a - (column / pivot) * pivot_row, a)
        )

    system = lax.fori_loop(0, members, eliminate, system)
    inner = jnp.sum(jnp.where(lane == members, system, 0.0), axis=1, keepdims=True)
    mean_weight = jnp.sum(system * inner, axis=0, keepdims=True)
    weights = mean_weight + jnp.sqrt(jnp.float32(members - 1.0)) * system
    own = jnp.logical_and(lane > members, lane <= 2 * members)
    weights = jnp.where(own, weights, 0.0)
    weights = weights - jnp.sum(weights, axis=1, keepdims=True) / members + 1.0 / members
    for j in range(members):
        column = jnp.sum(jnp.where(lane == members + 1 + j, weights, 0.0), axis=1, keepdims=True)
        spread[j] = jnp.broadcast_to(column, (members, LANES))

    for c in range(chunks):
        if c > 0:
            arrived(got.at[c, pl.ds(0, members - 1)], fore_recv.at[c])

        def update(m, carry):
            for q in range(width // LANES):
                part = pl.ds(q * LANES, LANES)
                acc = None
                for j in range(members):
                    term = spread[j, pl.ds(m, 1), :] * got[c, j, :, part]
                    acc = term if acc is None else acc + term
                reply[c, m, :, part] = jnp.where(
                    tile_mask[:, part] > 0, acc, got[c, m, :, part]
                )
            return carry

        lax.fori_loop(0, members, update, 0)

        def send_reply(i, carry):
            peer = lax.rem(me + i, members)
            pltpu.make_async_remote_copy(
                reply.at[c, peer], back.at[c, me], reply_send, reply_recv.at[c],
                device_id={"member": peer}, device_id_type=MESH,
            ).start()
            return carry

        lax.fori_loop(1, members, send_reply, 0)
        back[c, me] = reply[c, me]

    for c in range(chunks):
        arrived(back.at[c, pl.ds(0, members - 1)], reply_recv.at[c])
        for k in range(per_chunk):
            for tile in range(members):
                out[c * per_chunk + k, tile * tile_rows : (tile + 1) * tile_rows] = back[
                    c, tile, k * tile_rows : (k + 1) * tile_rows
                ]

    blocks = (slice(None), pl.ds(0, members - 1))
    arrived(sent.at[blocks], fore_send)
    arrived(reply.at[blocks], reply_send)
    arrived(sums_in.at[pl.ds(0, members - 1)], sums_send)

    @pl.when(jnp.logical_not(first))
    def _():
        for copy in to_upper:
            copy.wait_send()

    @pl.when(jnp.logical_not(last))
    def _():
        for copy in to_lower:
            copy.wait_send()


def shards(
    starting_tracer_fields, surface_exchange_inputs, diffusivity, mixing, land_mask,
    obs_index, obs_count, obs_value, obs_error,
):
    members = lax.axis_size("member")
    domains = lax.axis_size("domain")
    _, fields, levels, rows, width = starting_tracer_fields.shape
    parts = fields * levels
    tile_rows = rows // members
    chunks = parts * tile_rows // SUB
    sums_width = pl.cdiv(2 * members + 1, LANES) * LANES
    halo_rows = pl.cdiv(2 * (levels + 1), SUB) * SUB
    tiles, slots = obs_index.shape[1:]
    f32, i32 = jnp.float32, jnp.int32
    vmem = pltpu.VMEM
    dma = pltpu.SemaphoreType.DMA
    window = 2 * SUB
    blocks = (chunks, members, SUB, width)
    anywhere = pl.BlockSpec(memory_space=pl.ANY)
    scalars = pl.BlockSpec(memory_space=pltpu.SMEM)
    result = pl.pallas_call(
        functools.partial(body, members, domains),
        out_shape=pltpu.VMEM((parts, rows, width), f32),
        in_specs=[anywhere] * 6 + [scalars] * 3,
        out_specs=pl.BlockSpec(memory_space=pltpu.VMEM),
        scratch_shapes=[
            vmem((parts, rows, width), f32),
            vmem((fields, rows, width), f32),
            vmem((rows + 2 * SUB, width), i32),
            vmem((tiles, slots), i32),
            vmem((tiles, slots), f32),
            vmem((tiles, slots), f32),
            vmem((parts, rows, width), f32),
            vmem((parts, rows, width), f32),
            vmem((5, rows, width), f32),
            vmem((2, fields, halo_rows, width), f32),
            vmem((2, fields, halo_rows, width), f32),
            vmem((parts, window, width), f32),
            vmem((parts, window, width), f32),
            vmem((fields, window, width), f32),
            vmem((5, window, width), f32),
            vmem(blocks, f32),
            vmem(blocks, f32),
            vmem((sums_width, width), f32),
            vmem((members, sums_width), f32),
            vmem((members, members, sums_width), f32),
            vmem((members, members, LANES), f32),
            vmem((SUB, width), f32),
            vmem(blocks, f32),
            vmem(blocks, f32),
            dma((8,)),
            dma((2, fields)),
            dma((2, fields)),
            dma,
            dma((chunks,)),
            dma,
            dma,
            dma,
            dma((chunks,)),
        ],
        compiler_params=pltpu.CompilerParams(
            collective_id=0, has_side_effects=True, vmem_limit_bytes=56 * 1024 * 1024
        ),
    )(
        starting_tracer_fields.reshape(parts, rows, width),
        surface_exchange_inputs.reshape(fields, rows, width),
        land_mask,
        obs_index.reshape(tiles, slots),
        obs_value.reshape(tiles, slots),
        obs_error.reshape(tiles, slots),
        obs_count.reshape(1, tiles),
        diffusivity,
        mixing,
    )
    return result.reshape(starting_tracer_fields.shape)


def solution(mesh):
    placed = (
        P("member", None, None, "domain", None),
        P("member", None, "domain", None),
        P(),
        P(),
        P(),
        P("domain", None, None),
        P("domain", None),
        P("domain", None, None),
        P("domain", None, None),
    )
    return jax.shard_map(
        shards,
        mesh=mesh,
        in_specs=placed,
        out_specs=P("member", None, None, "domain", None),
        check_vma=False,
    )
```
